32 devices in a mesh: fits: 2 (over y), tm: 4 (over z), space: 4 (over x, core).
Axes of the slice: x: 2, y: 2, z: 4, core: 2. Of those that a mesh axis runs over, the one named last changes fastest.
Arguments:
- coupling: float32 [16, 4, 384, 384], P(('fits', 'tm'), 'space'), parts along dimension 0, may hold values from -0.034701105 to 1.0347011, as said below
- schur_inverse: float32 [16, 4, 384, 384], P(('fits', 'tm'), 'space'), parts along dimension 0, may hold values from -0.052051657 to 1.0720517, as said below
- entry_rows: int32 [16, 4, 2048], P(('fits', 'tm'), 'space'), parts along dimension 0, may hold values from 0 to 383
- entry_shift: int32 [16, 4, 2048], P(('fits', 'tm'), 'space'), parts along dimension 0, may hold values from -3 to 3
- entry_hyper: int32 [16, 4, 2048], P(('fits', 'tm'), 'space'), parts along dimension 0, may hold values from 0 to 3
- entry_values: float32 [16, 4, 2048], P(('fits', 'tm'), 'space'), parts along dimension 0, may hold values from -0.3125 to 0.3125
Outputs:
- marginal_cov: float32 [16, 4, 384, 384], P(('fits', 'tm'), 'space'), parts along dimension 0
- gradient: float32 [8], P('fits'), parts along dimension 0
The draws below stay inside these ranges and needn't reach their ends.
There are 2 independent parts, one for each index of `fits`. The reference program is written for one: setup_inputs(seed, part) draws one part's arguments, and reference() takes and returns one part's arrays. A program takes and returns all parts, laid end to end along the dimension named above; each array names one. Nothing has to cross between parts.
Inputs may be any that keep to these rules, and one draw needn't show every extreme that they name: Every block of coupling has entries within the stated range. Every block of schur_inverse is symmetric positive definite.
All inputs are finite; a program needn't handle non-finite values.
Results may differ from the reference program's by a relative error of at most 0.0001.
Values sent between devices are 32-bit elements; how exact they have to be, the bound alone decides.
A program may use at most 128 MiB of HBM per device.

```python
import jax
import jax.numpy as jnp
from jax import lax

SN = 384
NENT = 2048
NHYP = 4
TIMES = 8
NSUP = 4


def channel_decay(key):
    first_key = jax.random.fold_in(key, 11)
    second_key = jax.random.fold_in(key, 12)
    spread = jax.random.uniform(first_key, (NSUP, SN), jnp.float32)
    lowest = 1.15 / TIMES
    highest = 0.15
    base_rate = jnp.exp(jnp.log(lowest) + spread * (jnp.log(highest) - jnp.log(lowest)))
    jitter = jax.random.uniform(second_key, (TIMES, NSUP, SN), jnp.float32, 0.7, 1.4)
    return jnp.exp(-base_rate[None] * jitter)


def draw_coupling(key, part):
    decay = channel_decay(key)
    noise_key = jax.random.fold_in(key, 13)
    noise = jnp.clip(jax.random.normal(noise_key, (TIMES, NSUP, SN, SN), jnp.float32), -4.0, 4.0)
    identity = jnp.eye(SN, dtype=jnp.float32)
    return noise * (0.17 / SN ** 0.5) + decay[..., None] * identity


def draw_schur_inverse(key, part):
    decay = channel_decay(key)
    scales = jnp.sqrt(1.0 - decay * decay + 0.02)
    noise_key = jax.random.fold_in(key, 14)
    noise = jnp.clip(jax.random.normal(noise_key, (TIMES, NSUP, SN, SN), jnp.float32), -4.0, 4.0)
    symmetric = jnp.clip((noise + jnp.swapaxes(noise, 2, 3)) * 0.70710678, -4.0, 4.0)
    identity = jnp.eye(SN, dtype=jnp.float32)
    inner = identity + symmetric * (0.25 / SN ** 0.5)
    return scales[..., :, None] * inner * scales[..., None, :]


def place_ends(result, rng, smallest, high):
    spot = [jax.random.randint(jax.random.fold_in(rng, axis), (), 0, length) for axis, length in enumerate(result.shape)]
    main_axis = result.shape.index(max(result.shape))
    next_to = spot[:main_axis] + [(spot[main_axis] + 1) % result.shape[main_axis]] + spot[main_axis + 1:]
    return result.at[tuple(spot)].set(smallest).at[tuple(next_to)].set(high)


def level_of(rng, dims, cuts, least, high):
    level = 1.0
    for dim, blocks in cuts:
        steps = jax.random.uniform(jax.random.fold_in(jax.random.fold_in(rng, 6), dim), (blocks,), jnp.float32, least / len(cuts), high / len(cuts))
        level = level * jnp.repeat(jnp.exp(steps), dims[dim] // blocks).reshape((-1,) + (1,) * (len(dims) - 1 - dim))
    return level


def bell_draw(own_key, extent, scale, limit, shards=(), kind=jnp.bfloat16):
    factor_of = level_of(own_key, extent, shards, -0.22, 0.18) if shards else 1.0
    values = jax.random.normal(own_key, extent, jnp.float32) * scale * factor_of
    return jnp.minimum(jnp.maximum(values, -limit), limit).astype(kind)


def setup_inputs(seed: int = 0, part: int = 0) -> dict:
    keys = jax.random.split(jax.random.key(seed), 7)
    part_keys = jax.random.split(jax.random.fold_in(keys[6], part), 7)
    return {
        "coupling": draw_coupling(jax.random.fold_in(jax.random.fold_in(keys[6], part), 71), part),
        "schur_inverse": draw_schur_inverse(jax.random.fold_in(jax.random.fold_in(keys[6], part), 71), part),
        "entry_rows": place_ends(jax.random.randint(part_keys[2], (TIMES, NSUP, NENT), 0, SN), jax.random.fold_in(part_keys[2], 1), 0, SN - 1).astype(jnp.int32),
        "entry_shift": place_ends(jax.random.randint(part_keys[3], (TIMES, NSUP, NENT), -3, 4), jax.random.fold_in(part_keys[3], 1), -3, 3).astype(jnp.int32),
        "entry_hyper": place_ends(jax.random.randint(part_keys[4], (TIMES, NSUP, NENT), 0, NHYP), jax.random.fold_in(part_keys[4], 1), 0, NHYP - 1).astype(jnp.int32),
        "entry_values": bell_draw(part_keys[5], (TIMES, NSUP, NENT), ((7 * NHYP) ** 0.5 * (TIMES * NSUP * NENT) ** -0.5), 0.3125, ((0, 4), (1, 4)), jnp.float32),
    }


def apply_map(coupling, schur_inverse, current):
    product = jnp.einsum('sij,sjk->sik', coupling, current, precision=lax.Precision.HIGHEST)
    return jnp.einsum('sik,slk->sil', product, coupling, precision=lax.Precision.HIGHEST) + schur_inverse


def reference(coupling, schur_inverse, entry_rows, entry_shift, entry_hyper, entry_values):
    def backward(carry, pair):
        fresh = apply_map(pair[0], pair[1], carry)
        return fresh, fresh

    start = jnp.zeros_like(schur_inverse[0])
    _, stacked = lax.scan(backward, start, (coupling[::-1], schur_inverse[::-1]))
    marginal_cov = stacked[::-1]
    columns = jnp.mod(entry_rows + entry_shift, SN).astype(jnp.int32)
    flat_index = (entry_rows * SN + columns).astype(jnp.int32)
    flattened = marginal_cov.reshape(TIMES, NSUP, SN * SN)
    picked = jnp.take_along_axis(flattened, flat_index, axis=2)
    one_hot = (entry_hyper[..., None] == jnp.arange(NHYP, dtype=jnp.int32)).astype(picked.dtype)
    gradient = -0.5 * jnp.sum((entry_values * picked)[..., None] * one_hot, axis=(0, 1, 2))
    return marginal_cov, gradient
```

```python
import functools

import jax
import jax.numpy as jnp
from jax import lax
from jax.experimental import pallas as pl
from jax.experimental.pallas import tpu as pltpu
from jax.sharding import PartitionSpec as P

NHYP = 4
REACH = 3
TILE = 128
MESH = pl.DeviceIdType.MESH
F32 = jnp.float32
BF16 = jnp.bfloat16
NN = (((1,), (0,)), ((), ()))
NT = (((1,), (1,)), ((), ()))


def split(x):
    hi = x.astype(BF16)
    return hi, (x - hi.astype(F32)).astype(BF16)


def product(a, b, dims):
    def one(x, y):
        return lax.dot_general(x, y, dims, preferred_element_type=F32)

    return one(a[0], b[0]) + (one(a[0], b[1]) + one(a[1], b[0]))


def kernel(
    coupling_hbm,
    schur_hbm,
    rows_ref,
    shift_ref,
    hyper_ref,
    values_ref,
    out_hbm,
    grad_ref,
    g_in,
    s_in,
    result,
    g_hi,
    g_lo,
    c_hi,
    c_lo,
    b_hi,
    b_lo,
    q_hi,
    q_lo,
    outgoing,
    incoming,
    weights,
    partials,
    load_sem,
    store_sem,
    send_sem,
    recv_sem,
    turn_sem,
    part_send,
    part_recv,
):
    steps = g_in.shape[0]
    order = g_in.shape[1]
    blocks = order // TILE
    devices, spaces = lax.axis_size("tm"), lax.axis_size("space")
    me, mine = lax.axis_index("tm"), lax.axis_index("space")
    group = devices * spaces
    rank = me * spaces + mine
    is_last = me == devices - 1
    staggered = spaces % 2 == 0 and spaces > 1

    def peer(k):
        other = lax.rem(rank + k, group)
        return other, {"tm": other // spaces, "space": lax.rem(other, spaces)}

    loads = []
    for p in range(steps - 1, -1, -1):
        for which, (source, target) in enumerate(((coupling_hbm, g_in), (schur_hbm, s_in))):
            copy = pltpu.make_async_copy(source.at[p, 0], target.at[p], load_sem.at[which, p])
            copy.start()
            loads.append(copy)

    barrier = pltpu.get_barrier_semaphore()

    def greet(k, carry):
        _, where = peer(k)
        pl.semaphore_signal(barrier, inc=1, device_id=where, device_id_type=MESH)
        return carry

    lax.fori_loop(1, group, greet, 0)

    for copy in loads:
        copy.wait()

    def band(i):
        return slice(i * TILE, (i + 1) * TILE)

    for p in range(steps):
        g_hi[p], g_lo[p] = split(g_in[p])

    def set_current(x):
        b_hi[...], b_lo[...] = split(x)

    def first_half(gh, gl, i):
        part = product((b_hi[band(i), :], b_lo[band(i), :]), (gh[...], gl[...]), NT)
        q_hi[band(i), :], q_lo[band(i), :] = split(part)

    def second_half(gh, gl, add, i):
        right = slice(i * TILE, order)
        part = product(
            (gh[band(i), :], gl[band(i), :]), (q_hi[:, right], q_lo[:, right]), NN
        )
        return part + add[band(i), right]

    def mirror(target):
        for i in range(blocks):
            for j in range(i + 1, blocks):
                target[band(j), band(i)] = target[band(i), band(j)].T

    def hop(i):
        region = (band(i), slice(i * TILE, order))
        return pltpu.make_async_remote_copy(
            src_ref=outgoing.at[region],
            dst_ref=incoming.at[region],
            send_sem=send_sem.at[i],
            recv_sem=recv_sem.at[i],
            device_id={"tm": me - 1},
            device_id_type=MESH,
        )

    set_current(s_in[steps - 1])
    result[steps - 1] = s_in[steps - 1]
    for p in range(steps - 2, -1, -1):
        for i in range(blocks):
            first_half(g_hi.at[p], g_lo.at[p], i)
        for i in range(blocks):
            result[p, band(i), i * TILE :] = second_half(g_hi.at[p], g_lo.at[p], s_in.at[p], i)
        if p > 0:
            mirror(result.at[p])
            set_current(result[p])

    pl.semaphore_wait(barrier, group - 1)

    if devices > 1:

        @pl.when(is_last)
        def _():
            for i in range(blocks):
                right = slice(i * TILE, order)
                outgoing[band(i), right] = result[0, band(i), right]
            if staggered:

                @pl.when(lax.rem(mine, 2) == 1)
                def _():
                    pl.semaphore_wait(turn_sem, 1)

            for i in range(blocks):
                hop(i).start()

        @pl.when(jnp.logical_not(is_last))
        def _():
            if steps > 1:
                joined = product(
                    (g_hi[0], g_lo[0]), (g_hi[1], g_lo[1]), NN
                )
                c_hi[...], c_lo[...] = split(joined)
                for p in range(2, steps):
                    joined = product((c_hi[...], c_lo[...]), (g_hi[p], g_lo[p]), NN)
                    c_hi[...], c_lo[...] = split(joined)
            else:
                c_hi[...], c_lo[...] = g_hi[0], g_lo[0]

    codes = NHYP * (2 * REACH + 1)
    padded = weights.shape[1]
    count = rows_ref.shape[2]
    for p in range(steps):
        code = (shift_ref[p] + REACH) * NHYP + hyper_ref[p]
        chosen = lax.broadcasted_iota(jnp.int32, (padded, count), 0) == code
        value = values_ref[p]
        parts = []
        rest = value
        for _ in range(3):
            piece = rest.astype(BF16).astype(F32)
            parts.append(jnp.where(chosen, piece, 0.0).astype(BF16))
            rest = rest - piece
        spread = jnp.concatenate(parts, axis=0)
        placed = lax.broadcasted_iota(jnp.int32, (order, count), 0) == rows_ref[p]
        onehot = jnp.where(placed, 1.0, 0.0).astype(BF16)
        sums = lax.dot_general(spread, onehot, NT, preferred_element_type=F32)
        weights[p] = sums[:padded] + sums[padded : 2 * padded] + sums[2 * padded :]

    if devices > 1:
        if staggered:

            @pl.when(jnp.logical_and(is_last, lax.rem(mine, 2) == 0))
            def _():
                for i in range(blocks):
                    hop(i).wait_send()
                pl.semaphore_signal(
                    turn_sem, inc=1, device_id={"space": mine + 1}, device_id_type=MESH
                )

            @pl.when(jnp.logical_and(is_last, lax.rem(mine, 2) == 1))
            def _():
                for i in range(blocks):
                    hop(i).wait_send()
        else:

            @pl.when(is_last)
            def _():
                for i in range(blocks):
                    hop(i).wait_send()

        @pl.when(jnp.logical_not(is_last))
        def _():
            for i in range(blocks):
                hop(i).wait_recv()
                for j in range(i, blocks):
                    block = incoming[band(i), band(j)]
                    b_hi[band(i), band(j)], b_lo[band(i), band(j)] = split(block)
                    if j > i:
                        b_hi[band(j), band(i)], b_lo[band(j), band(i)] = split(block.T)
                first_half(c_hi, c_lo, i)
            for i in range(blocks):
                right = slice(i * TILE, order)
                fresh = second_half(c_hi, c_lo, result.at[0], i)
                result[0, band(i), right] = fresh

                @pl.when(me > 0)
                def _():
                    outgoing[band(i), right] = fresh
                    hop(i).start()

            for p in range(steps - 1, 0, -1):
                for i in range(blocks):
                    first_half(g_hi.at[p], g_lo.at[p], i)
                for i in range(blocks):
                    result[p, band(i), i * TILE :] = second_half(
                        g_hi.at[p], g_lo.at[p], s_in.at[p], i
                    )
                mirror(result.at[p])
                if p > 1:
                    set_current(result[p])

    if steps > 1 or devices > 1:
        mirror(result.at[0])

    stores = []
    for p in range(steps):
        copy = pltpu.make_async_copy(result.at[p], out_hbm.at[p, 0], store_sem.at[p])
        copy.start()
        stores.append(copy)

    def diagonals(p):
        pieces = []
        for b in range(blocks):
            above = (b * TILE - 8) % order
            below = (b + 1) * TILE % order
            strips = (
                (result[p, above : above + 8, band(b)], -8, 8),
                (result[p, band(b), band(b)], 0, TILE),
                (result[p, below : below + 8, band(b)], TILE, 8),
            )
            lines = [jnp.zeros((1, TILE), F32) for _ in range(2 * REACH + 1)]
            for block, base, height in strips:
                row = lax.broadcasted_iota(jnp.int32, (height, TILE), 0) + base
                offset = row - lax.broadcasted_iota(jnp.int32, (height, TILE), 1)
                for d in range(2 * REACH + 1):
                    lines[d] = lines[d] + jnp.sum(
                        jnp.where(offset == d - REACH, block, 0.0), axis=0, keepdims=True
                    )
            pieces.append(lines)
        return pieces

    total = jnp.zeros((8, TILE), F32)
    group_of = lax.broadcasted_iota(jnp.int32, (padded, TILE), 0) // NHYP
    for p in range(steps):
        for b, lines in enumerate(diagonals(p)):
            matched = jnp.zeros((padded, TILE), F32)
            for d in range(2 * REACH + 1):
                matched = jnp.where(group_of == d, lines[d], matched)
            terms = matched * weights[p, :, band(b)]
            for k in range(padded // 8):
                total = total + terms[8 * k : 8 * (k + 1)]
    partials[rank] = total

    def exchange(k):
        other, where = peer(k)
        return pltpu.make_async_remote_copy(
            src_ref=partials.at[rank],
            dst_ref=partials.at[rank],
            send_sem=part_send.at[k],
            recv_sem=part_recv.at[rank],
            device_id=where,
            device_id_type=MESH,
        )

    def start_exchange(k, carry):
        exchange(k).start()
        return carry

    lax.fori_loop(1, group, start_exchange, 0)

    def take(k, carry):
        other, where = peer(k)
        pltpu.make_async_remote_copy(
            src_ref=partials.at[other],
            dst_ref=partials.at[other],
            send_sem=part_send.at[k],
            recv_sem=part_recv.at[other],
            device_id=where,
            device_id_type=MESH,
        ).wait_recv()
        return carry

    lax.fori_loop(1, group, take, 0)
    everything = jnp.sum(partials[...], axis=0)
    everything = everything[:NHYP] + everything[NHYP : 2 * NHYP]
    for k in range(NHYP):
        grad_ref[k] = -0.5 * jnp.sum(everything[k : k + 1])

    def finish_exchange(k, carry):
        exchange(k).wait_send()
        return carry

    lax.fori_loop(1, group, finish_exchange, 0)
    if devices > 1:

        @pl.when(jnp.logical_and(me > 0, jnp.logical_not(is_last)))
        def _():
            for i in range(blocks):
                hop(i).wait_send()

    for copy in stores:
        copy.wait()


def on_device(group, coupling, schur_inverse, entry_rows, entry_shift, entry_hyper, entry_values):
    steps, _, order, _ = coupling.shape
    blocks = order // TILE
    whole = pl.BlockSpec(memory_space=pltpu.VMEM)
    apart = pl.BlockSpec(memory_space=pl.ANY)
    padded = 32
    return pl.pallas_call(
        kernel,
        out_shape=(
            jax.ShapeDtypeStruct(coupling.shape, F32),
            jax.ShapeDtypeStruct((NHYP,), F32),
        ),
        in_specs=[apart, apart, whole, whole, whole, whole],
        out_specs=(apart, pl.BlockSpec(memory_space=pltpu.SMEM)),
        scratch_shapes=[
            pltpu.VMEM((steps, order, order), F32),
            pltpu.VMEM((steps, order, order), F32),
            pltpu.VMEM((steps, order, order), F32),
            pltpu.VMEM((steps, order, order), BF16),
            pltpu.VMEM((steps, order, order), BF16),
            pltpu.VMEM((order, order), BF16),
            pltpu.VMEM((order, order), BF16),
            pltpu.VMEM((order, order), BF16),
            pltpu.VMEM((order, order), BF16),
            pltpu.VMEM((order, order), BF16),
            pltpu.VMEM((order, order), BF16),
            pltpu.VMEM((order, order), F32),
            pltpu.VMEM((order, order), F32),
            pltpu.VMEM((steps, padded, order), F32),
            pltpu.VMEM((group, 8, TILE), F32),
            pltpu.SemaphoreType.DMA((2, steps)),
            pltpu.SemaphoreType.DMA((steps,)),
            pltpu.SemaphoreType.DMA((blocks,)),
            pltpu.SemaphoreType.DMA((blocks,)),
            pltpu.SemaphoreType.REGULAR,
            pltpu.SemaphoreType.DMA((group,)),
            pltpu.SemaphoreType.DMA((group,)),
        ],
        compiler_params=pltpu.CompilerParams(collective_id=0, has_side_effects=True),
    )(coupling, schur_inverse, entry_rows, entry_shift, entry_hyper, entry_values)


def solution(mesh):
    group = mesh.shape["tm"] * mesh.shape["space"]
    in_specs = (
        P(("fits", "tm"), "space", None, None),
        P(("fits", "tm"), "space", None, None),
        P(("fits", "tm"), "space", None),
        P(("fits", "tm"), "space", None),
        P(("fits", "tm"), "space", None),
        P(("fits", "tm"), "space", None),
    )
    out_specs = (P(("fits", "tm"), "space", None, None), P("fits"))
    return jax.shard_map(
        functools.partial(on_device, group),
        mesh=mesh,
        in_specs=in_specs,
        out_specs=out_specs,
        check_vma=False,
    )
```

```python
import functools

import jax
import jax.numpy as jnp
from jax import lax
from jax.experimental import pallas as pl
from jax.experimental.pallas import tpu as pltpu
from jax.sharding import PartitionSpec as P

NHYP = 4
REACH = 3
TILE = 128
MESH = pl.DeviceIdType.MESH
F32 = jnp.float32
BF16 = jnp.bfloat16
OUT_TYPE = pltpu.VMEM
NN = (((1,), (0,)), ((), ()))
NT = (((1,), (1,)), ((), ()))


def split(x):
    hi = x.astype(BF16)
    return hi, (x - hi.astype(F32)).astype(BF16)


def product(a, b, dims):
    def one(x, y):
        return lax.dot_general(x, y, dims, preferred_element_type=F32)

    return one(a[0], b[0]) + (one(a[0], b[1]) + one(a[1], b[0]))


def kernel(
    coupling_hbm,
    schur_hbm,
    rows_hbm,
    shift_hbm,
    hyper_hbm,
    values_hbm,
    out_ref,
    grad_ref,
    g_in,
    s_in,
    rows_ref,
    shift_ref,
    hyper_ref,
    values_ref,
    g_hi,
    g_lo,
    c_hi,
    c_lo,
    b_hi,
    b_lo,
    q_hi,
    q_lo,
    out_a,
    out_b,
    out_c,
    in_a,
    in_b,
    in_c,
    weights,
    partials,
    load_sem,
    entry_sem,
    send_sem,
    recv_sem,
    turn_sem,
    part_send,
    part_recv,
):
    steps = g_in.shape[0]
    order = g_in.shape[1]
    blocks = order // TILE
    devices, spaces = lax.axis_size("tm"), lax.axis_size("space")
    me, mine = lax.axis_index("tm"), lax.axis_index("space")
    group = devices * spaces
    rank = me * spaces + mine
    is_last = me == devices - 1
    staggered = spaces % 2 == 0 and spaces > 1
    goes_first = lax.rem(mine, 2) == 0 if staggered else mine >= 0

    def peer(k):
        other = lax.rem(rank + k, group)
        return other, {"tm": other // spaces, "space": lax.rem(other, spaces)}

    result = out_ref.at[:, 0]
    sources = (coupling_hbm, schur_hbm)
    targets = (g_in, s_in)

    def load(which, p):
        return pltpu.make_async_copy(
            sources[which].at[p, 0], targets[which].at[p], load_sem.at[which, p]
        )

    order_of_loads = [(1, steps - 1)]
    for p in range(steps - 2, -1, -1):
        order_of_loads += [(0, p), (1, p)]
    order_of_loads.append((0, steps - 1))
    for which, p in order_of_loads:
        load(which, p).start()
    entries = []
    for k, (source, target) in enumerate(
        (
            (rows_hbm, rows_ref),
            (shift_hbm, shift_ref),
            (hyper_hbm, hyper_ref),
            (values_hbm, values_ref),
        )
    ):
        copy = pltpu.make_async_copy(source, target, entry_sem.at[k])
        copy.start()
        entries.append(copy)

    barrier = pltpu.get_barrier_semaphore()

    def greet(k, carry):
        _, where = peer(k)
        pl.semaphore_signal(barrier, inc=1, device_id=where, device_id_type=MESH)
        return carry

    lax.fori_loop(1, group, greet, 0)

    def band(i):
        return slice(i * TILE, (i + 1) * TILE)

    def set_current(x):
        b_hi[...], b_lo[...] = split(x)

    def first_half(gh, gl, i):
        part = product((b_hi[band(i), :], b_lo[band(i), :]), (gh[...], gl[...]), NT)
        q_hi[band(i), :], q_lo[band(i), :] = split(part)

    def second_half(gh, gl, add, i):
        right = slice(i * TILE, order)
        part = product(
            (gh[band(i), :], gl[band(i), :]), (q_hi[:, right], q_lo[:, right]), NN
        )
        return part + add[band(i), right]

    def mirror(target):
        for i in range(blocks):
            for j in range(i + 1, blocks):
                target[band(j), band(i)] = target[band(i), band(j)].T

    chunks = ((out_a, in_a), (out_b, in_b), (out_c, in_c))

    def hop(i):
        return pltpu.make_async_remote_copy(
            src_ref=chunks[i][0],
            dst_ref=chunks[i][1],
            send_sem=send_sem.at[i],
            recv_sem=recv_sem.at[i],
            device_id={"tm": me - 1},
            device_id_type=MESH,
        )

    half = TILE // 2

    def places(height=TILE):
        down = lax.broadcasted_iota(jnp.int32, (height, TILE), 0)
        return down, lax.broadcasted_iota(jnp.int32, (height, TILE), 1)

    def diagonal_of(x):
        down, across = places()
        return jnp.sum(jnp.where(across == down, x, 0.0), axis=0, keepdims=True)

    def pack(i, source):
        if i == 0:
            out_a[...] = source[band(0), TILE:]
        elif i == 1:
            down, across = places()
            second = source[band(1), band(1)]
            out_b[:TILE, :TILE] = jnp.where(across >= down, source[band(0), band(0)], second.T)
            out_b[:TILE, TILE:] = source[band(1), band(2)]
            line = jnp.broadcast_to(diagonal_of(second), (8, TILE))
            out_b[TILE:, :] = jnp.concatenate([line, line], axis=1)
        else:
            down, across = places(half)
            third = source[band(2), band(2)]
            turned = pltpu.roll(third.T, half, 1)
            out_c[:half, :] = jnp.where(across >= down, third[:half], turned[half:])
            out_c[half:, :] = jnp.broadcast_to(diagonal_of(third), (8, TILE))

    def put(i, j, block):
        b_hi[band(i), band(j)], b_lo[band(i), band(j)] = split(block)
        if i != j:
            b_hi[band(j), band(i)], b_lo[band(j), band(i)] = split(block.T)

    def unpack(i):
        if i == 0:
            put(0, 1, in_a[:, :TILE])
            put(0, 2, in_a[:, TILE:])
        elif i == 1:
            down, across = places()
            upper, diagonal = across >= down, across == down
            shared = in_b[:TILE, :TILE]
            turned = shared.T
            put(0, 0, jnp.where(upper, shared, turned))
            second = jnp.where(upper, turned, shared)
            put(1, 1, jnp.where(diagonal, in_b[TILE : TILE + 1, :TILE], second))
            put(1, 2, in_b[:TILE, TILE:])
        else:
            top = in_c[:half, :]
            corner = pltpu.roll(top, half, 1)
            low, along = places(half)
            one_side = jnp.concatenate(
                [
                    jnp.where(along >= low, top, 0.0),
                    jnp.where(
                        jnp.logical_and(along >= half, along < low + half), corner, 0.0
                    ),
                ],
                axis=0,
            )
            down, across = places()
            diagonal = across == down
            other = jnp.where(diagonal, 0.0, one_side)
            third = one_side + other.T
            third = jnp.where(diagonal, in_c[half : half + 1, :], third)
            put(2, 2, third)

    load(1, steps - 1).wait()
    set_current(s_in[steps - 1])
    result[steps - 1] = s_in[steps - 1]
    for p in range(steps - 2, -1, -1):
        load(0, p).wait()
        g_hi[p], g_lo[p] = split(g_in[p])
        for i in range(blocks):
            first_half(g_hi.at[p], g_lo.at[p], i)
        load(1, p).wait()
        for i in range(blocks):
            result[p, band(i), i * TILE :] = second_half(g_hi.at[p], g_lo.at[p], s_in.at[p], i)
            if p == 0 and devices > 1:
                if i == 0:
                    pl.semaphore_wait(barrier, group - 1)

                @pl.when(is_last)
                def _():
                    pack(i, result.at[0])

                @pl.when(jnp.logical_and(is_last, goes_first))
                def _():
                    hop(i).start()
        if p > 0:
            mirror(result.at[p])
            set_current(result[p])
    if steps == 1 or devices == 1:
        pl.semaphore_wait(barrier, group - 1)

    if devices > 1:
        if steps == 1:

            @pl.when(is_last)
            def _():
                for i in range(blocks):
                    pack(i, result.at[0])

            @pl.when(jnp.logical_and(is_last, goes_first))
            def _():
                for i in range(blocks):
                    hop(i).start()

        @pl.when(jnp.logical_and(is_last, goes_first))
        def _():
            for i in range(blocks):
                if staggered and i == blocks - 1:
                    pl.semaphore_signal(
                        turn_sem, inc=1, device_id={"space": mine + 1}, device_id_type=MESH
                    )
                hop(i).wait_send()

        if staggered:

            @pl.when(jnp.logical_and(is_last, jnp.logical_not(goes_first)))
            def _():
                pl.semaphore_wait(turn_sem, 1)
                for i in range(blocks):
                    hop(i).start()

    load(0, steps - 1).wait()
    g_hi[steps - 1], g_lo[steps - 1] = split(g_in[steps - 1])
    if devices > 1:

        @pl.when(jnp.logical_not(is_last))
        def _():
            c_hi[...], c_lo[...] = g_hi[0], g_lo[0]
            for p in range(1, steps):
                joined = product((c_hi[...], c_lo[...]), (g_hi[p], g_lo[p]), NN)
                c_hi[...], c_lo[...] = split(joined)

    for copy in entries:
        copy.wait()

    codes = NHYP * (2 * REACH + 1)
    padded = weights.shape[1]
    count = rows_ref.shape[2]
    for p in range(steps):
        code = (shift_ref[p] + REACH) * NHYP + hyper_ref[p]
        chosen = lax.broadcasted_iota(jnp.int32, (padded, count), 0) == code
        value = values_ref[p]
        parts = []
        rest = value
        for _ in range(3):
            piece = rest.astype(BF16).astype(F32)
            parts.append(jnp.where(chosen, piece, 0.0).astype(BF16))
            rest = rest - piece
        spread = jnp.concatenate(parts, axis=0)
        placed = lax.broadcasted_iota(jnp.int32, (order, count), 0) == rows_ref[p]
        onehot = jnp.where(placed, 1.0, 0.0).astype(BF16)
        sums = lax.dot_general(spread, onehot, NT, preferred_element_type=F32)
        weights[p] = sums[:padded] + sums[padded : 2 * padded] + sums[2 * padded :]

    if devices > 1:

        @pl.when(jnp.logical_not(is_last))
        def _():
            for i in range(blocks):
                hop(i).wait_recv()
                unpack(i)
                if i == 1:
                    first_half(c_hi, c_lo, 0)
                if i > 0:
                    first_half(c_hi, c_lo, i)
            for i in range(blocks):
                right = slice(i * TILE, order)
                fresh = second_half(c_hi, c_lo, result.at[0], i)
                result[0, band(i), right] = fresh

                @pl.when(me > 0)
                def _():
                    pack(i, result.at[0])
                    hop(i).start()

            for p in range(steps - 1, 0, -1):
                for i in range(blocks):
                    first_half(g_hi.at[p], g_lo.at[p], i)
                for i in range(blocks):
                    result[p, band(i), i * TILE :] = second_half(
                        g_hi.at[p], g_lo.at[p], s_in.at[p], i
                    )
                mirror(result.at[p])
                if p > 1:
                    set_current(result[p])

    if steps > 1 or devices > 1:
        mirror(result.at[0])

    def diagonals(p):
        pieces = []
        for b in range(blocks):
            above = (b * TILE - 8) % order
            below = (b + 1) * TILE % order
            strips = (
                (result[p, above : above + 8, band(b)], -8, 8),
                (result[p, band(b), band(b)], 0, TILE),
                (result[p, below : below + 8, band(b)], TILE, 8),
            )
            lines = [jnp.zeros((1, TILE), F32) for _ in range(2 * REACH + 1)]
            for block, base, height in strips:
                row = lax.broadcasted_iota(jnp.int32, (height, TILE), 0) + base
                offset = row - lax.broadcasted_iota(jnp.int32, (height, TILE), 1)
                for d in range(2 * REACH + 1):
                    lines[d] = lines[d] + jnp.sum(
                        jnp.where(offset == d - REACH, block, 0.0), axis=0, keepdims=True
                    )
            pieces.append(lines)
        return pieces

    total = jnp.zeros((8, TILE), F32)
    group_of = lax.broadcasted_iota(jnp.int32, (padded, TILE), 0) // NHYP
    for p in range(steps):
        for b, lines in enumerate(diagonals(p)):
            matched = jnp.zeros((padded, TILE), F32)
            for d in range(2 * REACH + 1):
                matched = jnp.where(group_of == d, lines[d], matched)
            terms = matched * weights[p, :, band(b)]
            for k in range(padded // 8):
                total = total + terms[8 * k : 8 * (k + 1)]
    partials[rank] = total

    def exchange(k):
        other, where = peer(k)
        return pltpu.make_async_remote_copy(
            src_ref=partials.at[rank],
            dst_ref=partials.at[rank],
            send_sem=part_send.at[k],
            recv_sem=part_recv.at[rank],
            device_id=where,
            device_id_type=MESH,
        )

    def start_exchange(k, carry):
        exchange(k).start()
        return carry

    lax.fori_loop(1, group, start_exchange, 0)

    def take(k, carry):
        other, where = peer(k)
        pltpu.make_async_remote_copy(
            src_ref=partials.at[other],
            dst_ref=partials.at[other],
            send_sem=part_send.at[k],
            recv_sem=part_recv.at[other],
            device_id=where,
            device_id_type=MESH,
        ).wait_recv()
        return carry

    lax.fori_loop(1, group, take, 0)
    everything = jnp.sum(partials[...], axis=0)
    everything = everything[:NHYP] + everything[NHYP : 2 * NHYP]
    for k in range(NHYP):
        grad_ref[k] = -0.5 * jnp.sum(everything[k : k + 1])

    def finish_exchange(k, carry):
        exchange(k).wait_send()
        return carry

    lax.fori_loop(1, group, finish_exchange, 0)
    if devices > 1:

        @pl.when(jnp.logical_and(me > 0, jnp.logical_not(is_last)))
        def _():
            for i in range(blocks):
                hop(i).wait_send()

        if staggered:

            @pl.when(jnp.logical_and(is_last, jnp.logical_not(goes_first)))
            def _():
                for i in range(blocks):
                    hop(i).wait_send()


def on_device(group, coupling, schur_inverse, entry_rows, entry_shift, entry_hyper, entry_values):
    steps, _, order, _ = coupling.shape
    blocks = order // TILE
    whole = pl.BlockSpec(memory_space=pltpu.VMEM)
    apart = pl.BlockSpec(memory_space=pl.ANY)
    padded = 32
    entries = (entry_rows, entry_shift, entry_hyper, entry_values)
    travelling = [
        pltpu.VMEM((TILE, 2 * TILE), F32),
        pltpu.VMEM((TILE + 8, 2 * TILE), F32),
        pltpu.VMEM((TILE // 2 + 8, TILE), F32),
    ]
    return pl.pallas_call(
        kernel,
        out_shape=(
            OUT_TYPE(coupling.shape, F32),
            jax.ShapeDtypeStruct((NHYP,), F32),
        ),
        in_specs=[apart] * 6,
        out_specs=(whole, pl.BlockSpec(memory_space=pltpu.SMEM)),
        scratch_shapes=[
            pltpu.VMEM((steps, order, order), F32),
            pltpu.VMEM((steps, order, order), F32),
            *[pltpu.VMEM(x.shape, x.dtype) for x in entries],
            pltpu.VMEM((steps, order, order), BF16),
            pltpu.VMEM((steps, order, order), BF16),
            pltpu.VMEM((order, order), BF16),
            pltpu.VMEM((order, order), BF16),
            pltpu.VMEM((order, order), BF16),
            pltpu.VMEM((order, order), BF16),
            pltpu.VMEM((order, order), BF16),
            pltpu.VMEM((order, order), BF16),
            *travelling,
            *travelling,
            pltpu.VMEM((steps, padded, order), F32),
            pltpu.VMEM((group, 8, TILE), F32),
            pltpu.SemaphoreType.DMA((2, steps)),
            pltpu.SemaphoreType.DMA((len(entries),)),
            pltpu.SemaphoreType.DMA((blocks,)),
            pltpu.SemaphoreType.DMA((blocks,)),
            pltpu.SemaphoreType.REGULAR,
            pltpu.SemaphoreType.DMA((group,)),
            pltpu.SemaphoreType.DMA((group,)),
        ],
        compiler_params=pltpu.CompilerParams(collective_id=0, has_side_effects=True),
    )(coupling, schur_inverse, entry_rows, entry_shift, entry_hyper, entry_values)


def solution(mesh):
    group = mesh.shape["tm"] * mesh.shape["space"]
    in_specs = (
        P(("fits", "tm"), "space", None, None),
        P(("fits", "tm"), "space", None, None),
        P(("fits", "tm"), "space", None),
        P(("fits", "tm"), "space", None),
        P(("fits", "tm"), "space", None),
        P(("fits", "tm"), "space", None),
    )
    out_specs = (P(("fits", "tm"), "space", None, None), P("fits"))
    return jax.shard_map(
        functools.partial(on_device, group),
        mesh=mesh,
        in_specs=in_specs,
        out_specs=out_specs,
        check_vma=False,
    )
```

```python
import functools

import jax
import jax.numpy as jnp
from jax import lax
from jax.experimental import pallas as pl
from jax.experimental.pallas import tpu as pltpu
from jax.sharding import PartitionSpec as P

NHYP = 4
REACH = 3
TILE = 128
MESH = pl.DeviceIdType.MESH
F32 = jnp.float32
BF16 = jnp.bfloat16
OUT_TYPE = pltpu.VMEM
NN = (((1,), (0,)), ((), ()))
NT = (((1,), (1,)), ((), ()))


def split(x):
    hi = x.astype(BF16)
    return hi, (x - hi.astype(F32)).astype(BF16)


def product(a, b, dims):
    def one(x, y):
        return lax.dot_general(x, y, dims, preferred_element_type=F32)

    return one(a[0], b[0]) + (one(a[0], b[1]) + one(a[1], b[0]))


def kernel(
    coupling_hbm,
    schur_hbm,
    rows_hbm,
    shift_hbm,
    hyper_hbm,
    values_hbm,
    out_ref,
    grad_ref,
    g_in,
    s_in,
    rows_ref,
    shift_ref,
    hyper_ref,
    values_ref,
    g_hi,
    g_lo,
    c_hi,
    c_lo,
    b_hi,
    b_lo,
    q_hi,
    q_lo,
    out_a,
    out_b,
    out_c,
    in_a,
    in_b,
    in_c,
    weights,
    adjoint,
    partials,
    load_sem,
    entry_sem,
    send_sem,
    recv_sem,
    turn_sem,
    part_send,
    part_recv,
):
    steps = g_in.shape[0]
    order = g_in.shape[1]
    blocks = order // TILE
    devices, spaces = lax.axis_size("tm"), lax.axis_size("space")
    me, mine = lax.axis_index("tm"), lax.axis_index("space")
    group = devices * spaces
    rank = me * spaces + mine
    is_last = me == devices - 1
    staggered = spaces % 2 == 0 and spaces > 1
    early = devices > 1 and steps <= 2
    goes_first = lax.rem(mine, 2) == 0 if staggered else mine >= 0

    def peer(k):
        other = lax.rem(rank + k, group)
        return other, {"tm": other // spaces, "space": lax.rem(other, spaces)}

    result = out_ref.at[:, 0]
    sources = (coupling_hbm, schur_hbm)
    targets = (g_in, s_in)

    def load(which, p):
        return pltpu.make_async_copy(
            sources[which].at[p, 0], targets[which].at[p], load_sem.at[which, p]
        )

    order_of_loads = [(1, steps - 1)]
    for p in range(steps - 2, -1, -1):
        order_of_loads += [(0, p), (1, p)]
    order_of_loads.append((0, steps - 1))
    for which, p in order_of_loads:
        load(which, p).start()
    entries = []
    for k, (source, target) in enumerate(
        (
            (rows_hbm, rows_ref),
            (shift_hbm, shift_ref),
            (hyper_hbm, hyper_ref),
            (values_hbm, values_ref),
        )
    ):
        copy = pltpu.make_async_copy(source, target, entry_sem.at[k])
        copy.start()
        entries.append(copy)

    barrier = pltpu.get_barrier_semaphore()

    def greet(k, carry):
        _, where = peer(k)
        pl.semaphore_signal(barrier, inc=1, device_id=where, device_id_type=MESH)
        return carry

    lax.fori_loop(1, group, greet, 0)

    def band(i):
        return slice(i * TILE, (i + 1) * TILE)

    def set_current(x):
        b_hi[...], b_lo[...] = split(x)

    def first_half(gh, gl, i):
        part = product((b_hi[band(i), :], b_lo[band(i), :]), (gh[...], gl[...]), NT)
        q_hi[band(i), :], q_lo[band(i), :] = split(part)

    def second_half(gh, gl, add, i):
        right = slice(i * TILE, order)
        part = product(
            (gh[band(i), :], gl[band(i), :]), (q_hi[:, right], q_lo[:, right]), NN
        )
        return part + add[band(i), right]

    def mirror(target):
        for i in range(blocks):
            for j in range(i + 1, blocks):
                target[band(j), band(i)] = target[band(i), band(j)].T

    chunks = ((out_a, in_a), (out_b, in_b), (out_c, in_c))

    def hop(i):
        return pltpu.make_async_remote_copy(
            src_ref=chunks[i][0],
            dst_ref=chunks[i][1],
            send_sem=send_sem.at[i],
            recv_sem=recv_sem.at[i],
            device_id={"tm": me - 1},
            device_id_type=MESH,
        )

    half = TILE // 2

    def places(height=TILE):
        down = lax.broadcasted_iota(jnp.int32, (height, TILE), 0)
        return down, lax.broadcasted_iota(jnp.int32, (height, TILE), 1)

    def diagonal_of(x):
        down, across = places()
        return jnp.sum(jnp.where(across == down, x, 0.0), axis=0, keepdims=True)

    def pack(i, source):
        if i == 0:
            out_a[...] = source[band(0), TILE:]
        elif i == 1:
            down, across = places()
            second = source[band(1), band(1)]
            out_b[:TILE, :TILE] = jnp.where(across >= down, source[band(0), band(0)], second.T)
            out_b[:TILE, TILE:] = source[band(1), band(2)]
            line = jnp.broadcast_to(diagonal_of(second), (8, TILE))
            out_b[TILE:, :] = jnp.concatenate([line, line], axis=1)
        else:
            down, across = places(half)
            third = source[band(2), band(2)]
            turned = pltpu.roll(third.T, half, 1)
            out_c[:half, :] = jnp.where(across >= down, third[:half], turned[half:])
            out_c[half:, :] = jnp.broadcast_to(diagonal_of(third), (8, TILE))

    def put(i, j, block):
        b_hi[band(i), band(j)], b_lo[band(i), band(j)] = split(block)
        if i != j:
            b_hi[band(j), band(i)], b_lo[band(j), band(i)] = split(block.T)

    def unpack(i):
        if i == 0:
            put(0, 1, in_a[:, :TILE])
            put(0, 2, in_a[:, TILE:])
        elif i == 1:
            down, across = places()
            upper, diagonal = across >= down, across == down
            shared = in_b[:TILE, :TILE]
            turned = shared.T
            put(0, 0, jnp.where(upper, shared, turned))
            second = jnp.where(upper, turned, shared)
            put(1, 1, jnp.where(diagonal, in_b[TILE : TILE + 1, :TILE], second))
            put(1, 2, in_b[:TILE, TILE:])
        else:
            top = in_c[:half, :]
            corner = pltpu.roll(top, half, 1)
            low, along = places(half)
            one_side = jnp.concatenate(
                [
                    jnp.where(along >= low, top, 0.0),
                    jnp.where(
                        jnp.logical_and(along >= half, along < low + half), corner, 0.0
                    ),
                ],
                axis=0,
            )
            down, across = places()
            diagonal = across == down
            other = jnp.where(diagonal, 0.0, one_side)
            third = one_side + other.T
            third = jnp.where(diagonal, in_c[half : half + 1, :], third)
            put(2, 2, third)

    load(1, steps - 1).wait()
    set_current(s_in[steps - 1])
    result[steps - 1] = s_in[steps - 1]
    for p in range(steps - 2, -1, -1):
        load(0, p).wait()
        g_hi[p], g_lo[p] = split(g_in[p])
        for i in range(blocks):
            first_half(g_hi.at[p], g_lo.at[p], i)
        load(1, p).wait()
        for i in range(blocks):
            result[p, band(i), i * TILE :] = second_half(g_hi.at[p], g_lo.at[p], s_in.at[p], i)
            if p == 0 and devices > 1:
                if i == 0:
                    pl.semaphore_wait(barrier, group - 1)

                @pl.when(is_last)
                def _():
                    pack(i, result.at[0])

                @pl.when(jnp.logical_and(is_last, goes_first))
                def _():
                    hop(i).start()
        if p > 0:
            mirror(result.at[p])
            set_current(result[p])
    if steps == 1 or devices == 1:
        pl.semaphore_wait(barrier, group - 1)

    if devices > 1:
        if steps == 1:

            @pl.when(is_last)
            def _():
                for i in range(blocks):
                    pack(i, result.at[0])

            @pl.when(jnp.logical_and(is_last, goes_first))
            def _():
                for i in range(blocks):
                    hop(i).start()

        @pl.when(jnp.logical_and(is_last, goes_first))
        def _():
            for i in range(blocks):
                if staggered and i == blocks - 1:
                    pl.semaphore_signal(
                        turn_sem, inc=1, device_id={"space": mine + 1}, device_id_type=MESH
                    )
                hop(i).wait_send()

        if staggered:

            @pl.when(jnp.logical_and(is_last, jnp.logical_not(goes_first)))
            def _():
                pl.semaphore_wait(turn_sem, 1)
                for i in range(blocks):
                    hop(i).start()

    load(0, steps - 1).wait()
    g_hi[steps - 1], g_lo[steps - 1] = split(g_in[steps - 1])
    if devices > 1:

        @pl.when(jnp.logical_not(is_last))
        def _():
            c_hi[...], c_lo[...] = g_hi[0], g_lo[0]
            for p in range(1, steps):
                joined = product((c_hi[...], c_lo[...]), (g_hi[p], g_lo[p]), NN)
                c_hi[...], c_lo[...] = split(joined)

    for copy in entries:
        copy.wait()

    codes = NHYP * (2 * REACH + 1)
    padded = weights.shape[1]
    count = rows_ref.shape[2]
    for p in range(steps):
        code = (shift_ref[p] + REACH) * NHYP + hyper_ref[p]
        chosen = lax.broadcasted_iota(jnp.int32, (padded, count), 0) == code
        value = values_ref[p]
        parts = []
        rest = value
        for _ in range(3):
            piece = rest.astype(BF16).astype(F32)
            parts.append(jnp.where(chosen, piece, 0.0).astype(BF16))
            rest = rest - piece
        spread = jnp.concatenate(parts, axis=0)
        placed = lax.broadcasted_iota(jnp.int32, (order, count), 0) == rows_ref[p]
        onehot = jnp.where(placed, 1.0, 0.0).astype(BF16)
        sums = lax.dot_general(spread, onehot, NT, preferred_element_type=F32)
        weights[p] = sums[:padded] + sums[padded : 2 * padded] + sums[2 * padded :]

    def diagonals(p):
        pieces = []
        for b in range(blocks):
            above = (b * TILE - 8) % order
            below = (b + 1) * TILE % order
            strips = (
                (result[p, above : above + 8, band(b)], -8, 8),
                (result[p, band(b), band(b)], 0, TILE),
                (result[p, below : below + 8, band(b)], TILE, 8),
            )
            lines = [jnp.zeros((1, TILE), F32) for _ in range(2 * REACH + 1)]
            for block, base, height in strips:
                row = lax.broadcasted_iota(jnp.int32, (height, TILE), 0) + base
                offset = row - lax.broadcasted_iota(jnp.int32, (height, TILE), 1)
                for d in range(2 * REACH + 1):
                    lines[d] = lines[d] + jnp.sum(
                        jnp.where(offset == d - REACH, block, 0.0), axis=0, keepdims=True
                    )
            pieces.append(lines)
        return pieces

    def direct_terms():
        total = jnp.zeros((8, TILE), F32)
        group_of = lax.broadcasted_iota(jnp.int32, (padded, TILE), 0) // NHYP
        for p in range(steps):
            for b, lines in enumerate(diagonals(p)):
                matched = jnp.zeros((padded, TILE), F32)
                for d in range(2 * REACH + 1):
                    matched = jnp.where(group_of == d, lines[d], matched)
                terms = matched * weights[p, :, band(b)]
                for k in range(padded // 8):
                    total = total + terms[8 * k : 8 * (k + 1)]
        return total

    def exchange(k):
        other, where = peer(k)
        return pltpu.make_async_remote_copy(
            src_ref=partials.at[rank],
            dst_ref=partials.at[rank],
            send_sem=part_send.at[k],
            recv_sem=part_recv.at[rank],
            device_id=where,
            device_id_type=MESH,
        )

    def start_exchange(k, carry):
        exchange(k).start()
        return carry

    def prepare():
        mirror(result.at[0])
        partials[rank] = direct_terms()
        down = lax.broadcasted_iota(jnp.int32, (order, order), 0)
        offset = down - lax.broadcasted_iota(jnp.int32, (order, order), 1)

        def for_hyper(k, carry):
            for p in range(steps):
                gains = (c_hi[...], c_lo[...]) if p == 0 else (g_hi[p], g_lo[p])
                spots = jnp.zeros((order, order), F32)
                for d in range(-REACH, REACH + 1):
                    line = weights[p, pl.ds((d + REACH) * NHYP + k, 1), :]
                    here = offset == d
                    if d != 0:
                        here = jnp.logical_or(here, offset == (d - order if d > 0 else d + order))
                    spots = jnp.where(here, line, spots)
                right = product(split(spots), gains, NN)
                both = product(split(right.T), gains, NN)
                adjoint[k] = both if p == 0 else adjoint[k] + both
            return carry

        lax.fori_loop(0, NHYP, for_hyper, 0)

    def finish_early():
        total = partials[rank]
        spot = lax.broadcasted_iota(jnp.int32, (8, TILE), 0)
        current = b_hi[...].astype(F32) + b_lo[...].astype(F32)
        for k in range(NHYP):
            line = jnp.sum(adjoint[k] * current, axis=0, keepdims=True)
            line = sum(line[:, band(i)] for i in range(blocks))
            total = total + jnp.where(spot == k, line, 0.0)
        partials[rank] = total
        lax.fori_loop(1, group, start_exchange, 0)

    if early:

        @pl.when(me == 0)
        def _():
            prepare()

    if devices > 1:

        @pl.when(jnp.logical_not(is_last))
        def _():
            for i in range(blocks):
                hop(i).wait_recv()
                unpack(i)
                if i == 1:
                    first_half(c_hi, c_lo, 0)
                if i > 0 and not (early and i == blocks - 1):
                    first_half(c_hi, c_lo, i)
            if early:

                @pl.when(me == 0)
                def _():
                    finish_early()

                first_half(c_hi, c_lo, blocks - 1)
            for i in range(blocks):
                right = slice(i * TILE, order)
                fresh = second_half(c_hi, c_lo, result.at[0], i)
                result[0, band(i), right] = fresh

                @pl.when(me > 0)
                def _():
                    pack(i, result.at[0])
                    hop(i).start()

            for p in range(steps - 1, 0, -1):
                for i in range(blocks):
                    first_half(g_hi.at[p], g_lo.at[p], i)
                for i in range(blocks):
                    result[p, band(i), i * TILE :] = second_half(
                        g_hi.at[p], g_lo.at[p], s_in.at[p], i
                    )
                mirror(result.at[p])
                if p > 1:
                    set_current(result[p])

    if steps > 1 or devices > 1:
        mirror(result.at[0])

    if early:

        @pl.when(me != 0)
        def _():
            partials[rank] = direct_terms()
            lax.fori_loop(1, group, start_exchange, 0)
    else:
        partials[rank] = direct_terms()
        lax.fori_loop(1, group, start_exchange, 0)

    def take(k, carry):
        other, where = peer(k)
        pltpu.make_async_remote_copy(
            src_ref=partials.at[other],
            dst_ref=partials.at[other],
            send_sem=part_send.at[k],
            recv_sem=part_recv.at[other],
            device_id=where,
            device_id_type=MESH,
        ).wait_recv()
        return carry

    lax.fori_loop(1, group, take, 0)
    everything = jnp.sum(partials[...], axis=0)
    everything = everything[:NHYP] + everything[NHYP : 2 * NHYP]
    for k in range(NHYP):
        grad_ref[k] = -0.5 * jnp.sum(everything[k : k + 1])

    def finish_exchange(k, carry):
        exchange(k).wait_send()
        return carry

    lax.fori_loop(1, group, finish_exchange, 0)
    if devices > 1:

        @pl.when(jnp.logical_and(me > 0, jnp.logical_not(is_last)))
        def _():
            for i in range(blocks):
                hop(i).wait_send()

        if staggered:

            @pl.when(jnp.logical_and(is_last, jnp.logical_not(goes_first)))
            def _():
                for i in range(blocks):
                    hop(i).wait_send()


def on_device(group, coupling, schur_inverse, entry_rows, entry_shift, entry_hyper, entry_values):
    steps, _, order, _ = coupling.shape
    blocks = order // TILE
    whole = pl.BlockSpec(memory_space=pltpu.VMEM)
    apart = pl.BlockSpec(memory_space=pl.ANY)
    padded = 32
    entries = (entry_rows, entry_shift, entry_hyper, entry_values)
    travelling = [
        pltpu.VMEM((TILE, 2 * TILE), F32),
        pltpu.VMEM((TILE + 8, 2 * TILE), F32),
        pltpu.VMEM((TILE // 2 + 8, TILE), F32),
    ]
    return pl.pallas_call(
        kernel,
        out_shape=(
            OUT_TYPE(coupling.shape, F32),
            jax.ShapeDtypeStruct((NHYP,), F32),
        ),
        in_specs=[apart] * 6,
        out_specs=(whole, pl.BlockSpec(memory_space=pltpu.SMEM)),
        scratch_shapes=[
            pltpu.VMEM((steps, order, order), F32),
            pltpu.VMEM((steps, order, order), F32),
            *[pltpu.VMEM(x.shape, x.dtype) for x in entries],
            pltpu.VMEM((steps, order, order), BF16),
            pltpu.VMEM((steps, order, order), BF16),
            pltpu.VMEM((order, order), BF16),
            pltpu.VMEM((order, order), BF16),
            pltpu.VMEM((order, order), BF16),
            pltpu.VMEM((order, order), BF16),
            pltpu.VMEM((order, order), BF16),
            pltpu.VMEM((order, order), BF16),
            *travelling,
            *travelling,
            pltpu.VMEM((steps, padded, order), F32),
            pltpu.VMEM((NHYP, order, order), F32),
            pltpu.VMEM((group, 8, TILE), F32),
            pltpu.SemaphoreType.DMA((2, steps)),
            pltpu.SemaphoreType.DMA((len(entries),)),
            pltpu.SemaphoreType.DMA((blocks,)),
            pltpu.SemaphoreType.DMA((blocks,)),
            pltpu.SemaphoreType.REGULAR,
            pltpu.SemaphoreType.DMA((group,)),
            pltpu.SemaphoreType.DMA((group,)),
        ],
        compiler_params=pltpu.CompilerParams(collective_id=0, has_side_effects=True),
    )(coupling, schur_inverse, entry_rows, entry_shift, entry_hyper, entry_values)


def solution(mesh):
    group = mesh.shape["tm"] * mesh.shape["space"]
    in_specs = (
        P(("fits", "tm"), "space", None, None),
        P(("fits", "tm"), "space", None, None),
        P(("fits", "tm"), "space", None),
        P(("fits", "tm"), "space", None),
        P(("fits", "tm"), "space", None),
        P(("fits", "tm"), "space", None),
    )
    out_specs = (P(("fits", "tm"), "space", None, None), P("fits"))
    return jax.shard_map(
        functools.partial(on_device, group),
        mesh=mesh,
        in_specs=in_specs,
        out_specs=out_specs,
        check_vma=False,
    )
```

```python
import functools

import jax
import jax.numpy as jnp
from jax import lax
from jax.experimental import pallas as pl
from jax.experimental.pallas import tpu as pltpu
from jax.sharding import PartitionSpec as P

NHYP = 4
REACH = 3
TILE = 128
MESH = pl.DeviceIdType.MESH
F32 = jnp.float32
BF16 = jnp.bfloat16
OUT_TYPE = pltpu.VMEM
NN = (((1,), (0,)), ((), ()))
NT = (((1,), (1,)), ((), ()))


def split(x):
    hi = x.astype(BF16)
    return hi, (x - hi.astype(F32)).astype(BF16)


def product(a, b, dims):
    def one(x, y):
        return lax.dot_general(x, y, dims, preferred_element_type=F32)

    return one(a[0], b[0]) + (one(a[0], b[1]) + one(a[1], b[0]))


def kernel(
    coupling_hbm,
    schur_hbm,
    rows_hbm,
    shift_hbm,
    hyper_hbm,
    values_hbm,
    out_ref,
    grad_ref,
    g_in,
    s_in,
    rows_ref,
    shift_ref,
    hyper_ref,
    values_ref,
    g_hi,
    g_lo,
    c_hi,
    c_lo,
    b_hi,
    b_lo,
    q_hi,
    q_lo,
    out_a,
    out_b,
    out_c,
    in_a,
    in_b,
    in_c,
    weights,
    adjoint,
    partials,
    load_sem,
    entry_sem,
    send_sem,
    recv_sem,
    turn_sem,
    part_send,
    part_recv,
):
    steps = g_in.shape[0]
    order = g_in.shape[1]
    blocks = order // TILE
    devices, spaces = lax.axis_size("tm"), lax.axis_size("space")
    me, mine = lax.axis_index("tm"), lax.axis_index("space")
    group = devices * spaces
    rank = me * spaces + mine
    is_last = me == devices - 1
    staggered = spaces % 2 == 0 and spaces > 1
    early = devices > 1 and steps <= 2
    goes_first = lax.rem(mine, 2) == 0 if staggered else mine >= 0

    def peer(k):
        other = lax.rem(rank + k, group)
        return other, {"tm": other // spaces, "space": lax.rem(other, spaces)}

    result = out_ref.at[:, 0]
    sources = (coupling_hbm, schur_hbm)
    targets = (g_in, s_in)

    def load(which, p):
        return pltpu.make_async_copy(
            sources[which].at[p, 0], targets[which].at[p], load_sem.at[which, p]
        )

    order_of_loads = [(1, steps - 1)]
    for p in range(steps - 2, -1, -1):
        order_of_loads += [(0, p), (1, p)]
    order_of_loads.append((0, steps - 1))
    for which, p in order_of_loads:
        load(which, p).start()
    entries = []
    for k, (source, target) in enumerate(
        (
            (rows_hbm, rows_ref),
            (shift_hbm, shift_ref),
            (hyper_hbm, hyper_ref),
            (values_hbm, values_ref),
        )
    ):
        copy = pltpu.make_async_copy(source, target, entry_sem.at[k])
        copy.start()
        entries.append(copy)

    barrier = pltpu.get_barrier_semaphore()

    def greet(k, carry):
        _, where = peer(k)
        pl.semaphore_signal(barrier, inc=1, device_id=where, device_id_type=MESH)
        return carry

    lax.fori_loop(1, group, greet, 0)

    def band(i):
        return slice(i * TILE, (i + 1) * TILE)

    def set_current(x):
        b_hi[...], b_lo[...] = split(x)

    def first_half(gh, gl, i):
        part = product((b_hi[band(i), :], b_lo[band(i), :]), (gh[...], gl[...]), NT)
        q_hi[band(i), :], q_lo[band(i), :] = split(part)

    def second_half(gh, gl, add, i):
        right = slice(i * TILE, order)
        part = product(
            (gh[band(i), :], gl[band(i), :]), (q_hi[:, right], q_lo[:, right]), NN
        )
        return part + add[band(i), right]

    def mirror(target):
        for i in range(blocks):
            for j in range(i + 1, blocks):
                target[band(j), band(i)] = target[band(i), band(j)].T

    chunks = ((out_a, in_a), (out_b, in_b), (out_c, in_c))

    def hop(i):
        return pltpu.make_async_remote_copy(
            src_ref=chunks[i][0],
            dst_ref=chunks[i][1],
            send_sem=send_sem.at[i],
            recv_sem=recv_sem.at[i],
            device_id={"tm": me - 1},
            device_id_type=MESH,
        )

    half = TILE // 2

    def places(height=TILE):
        down = lax.broadcasted_iota(jnp.int32, (height, TILE), 0)
        return down, lax.broadcasted_iota(jnp.int32, (height, TILE), 1)

    def diagonal_of(x):
        down, across = places()
        return jnp.sum(jnp.where(across == down, x, 0.0), axis=0, keepdims=True)

    def pack(i, source):
        if i == 0:
            out_a[...] = source[band(0), TILE:]
        elif i == 1:
            down, across = places()
            second = source[band(1), band(1)]
            out_b[:TILE, :TILE] = jnp.where(across >= down, source[band(0), band(0)], second.T)
            out_b[:TILE, TILE:] = source[band(1), band(2)]
            line = jnp.broadcast_to(diagonal_of(second), (8, TILE))
            out_b[TILE:, :] = jnp.concatenate([line, line], axis=1)
        else:
            down, across = places(half)
            third = source[band(2), band(2)]
            turned = pltpu.roll(third.T, half, 1)
            out_c[:half, :] = jnp.where(across >= down, third[:half], turned[half:])
            out_c[half:, :] = jnp.broadcast_to(diagonal_of(third), (8, TILE))

    def put(i, j, block):
        b_hi[band(i), band(j)], b_lo[band(i), band(j)] = split(block)
        if i != j:
            b_hi[band(j), band(i)], b_lo[band(j), band(i)] = split(block.T)

    def unpack(i):
        if i == 0:
            put(0, 1, in_a[:, :TILE])
            put(0, 2, in_a[:, TILE:])
        elif i == 1:
            down, across = places()
            upper, diagonal = across >= down, across == down
            shared = in_b[:TILE, :TILE]
            turned = shared.T
            put(0, 0, jnp.where(upper, shared, turned))
            second = jnp.where(upper, turned, shared)
            put(1, 1, jnp.where(diagonal, in_b[TILE : TILE + 1, :TILE], second))
            put(1, 2, in_b[:TILE, TILE:])
        else:
            top = in_c[:half, :]
            corner = pltpu.roll(top, half, 1)
            low, along = places(half)
            one_side = jnp.concatenate(
                [
                    jnp.where(along >= low, top, 0.0),
                    jnp.where(
                        jnp.logical_and(along >= half, along < low + half), corner, 0.0
                    ),
                ],
                axis=0,
            )
            down, across = places()
            diagonal = across == down
            other = jnp.where(diagonal, 0.0, one_side)
            third = one_side + other.T
            third = jnp.where(diagonal, in_c[half : half + 1, :], third)
            put(2, 2, third)

    load(1, steps - 1).wait()
    set_current(s_in[steps - 1])
    result[steps - 1] = s_in[steps - 1]
    for p in range(steps - 2, -1, -1):
        load(0, p).wait()
        g_hi[p], g_lo[p] = split(g_in[p])
        for i in range(blocks):
            first_half(g_hi.at[p], g_lo.at[p], i)
        load(1, p).wait()
        for i in range(blocks):
            result[p, band(i), i * TILE :] = second_half(g_hi.at[p], g_lo.at[p], s_in.at[p], i)
            if p == 0 and devices > 1:
                if i == 0:
                    pl.semaphore_wait(barrier, group - 1)

                @pl.when(is_last)
                def _():
                    pack(i, result.at[0])

                @pl.when(jnp.logical_and(is_last, goes_first))
                def _():
                    hop(i).start()
        if p > 0:
            mirror(result.at[p])
            set_current(result[p])
    if steps == 1 or devices == 1:
        pl.semaphore_wait(barrier, group - 1)

    if devices > 1:
        if steps == 1:

            @pl.when(is_last)
            def _():
                for i in range(blocks):
                    pack(i, result.at[0])

            @pl.when(jnp.logical_and(is_last, goes_first))
            def _():
                for i in range(blocks):
                    hop(i).start()

        @pl.when(jnp.logical_and(is_last, goes_first))
        def _():
            for i in range(blocks):
                if staggered and i == 1:
                    pl.semaphore_signal(
                        turn_sem, inc=1, device_id={"space": mine + 1}, device_id_type=MESH
                    )
                hop(i).wait_send()

        if staggered:

            @pl.when(jnp.logical_and(is_last, jnp.logical_not(goes_first)))
            def _():
                pl.semaphore_wait(turn_sem, 1)
                for i in range(blocks):
                    hop(i).start()

    load(0, steps - 1).wait()
    g_hi[steps - 1], g_lo[steps - 1] = split(g_in[steps - 1])
    if devices > 1:

        @pl.when(jnp.logical_not(is_last))
        def _():
            c_hi[...], c_lo[...] = g_hi[0], g_lo[0]
            for p in range(1, steps):
                joined = product((c_hi[...], c_lo[...]), (g_hi[p], g_lo[p]), NN)
                c_hi[...], c_lo[...] = split(joined)

    for copy in entries:
        copy.wait()

    codes = NHYP * (2 * REACH + 1)
    padded = weights.shape[1]
    count = rows_ref.shape[2]
    for p in range(steps):
        code = (shift_ref[p] + REACH) * NHYP + hyper_ref[p]
        chosen = lax.broadcasted_iota(jnp.int32, (padded, count), 0) == code
        value = values_ref[p]
        parts = []
        rest = value
        for _ in range(3):
            piece = rest.astype(BF16).astype(F32)
            parts.append(jnp.where(chosen, piece, 0.0).astype(BF16))
            rest = rest - piece
        spread = jnp.concatenate(parts, axis=0)
        placed = lax.broadcasted_iota(jnp.int32, (order, count), 0) == rows_ref[p]
        onehot = jnp.where(placed, 1.0, 0.0).astype(BF16)
        sums = lax.dot_general(spread, onehot, NT, preferred_element_type=F32)
        weights[p] = sums[:padded] + sums[padded : 2 * padded] + sums[2 * padded :]

    def diagonals(p):
        pieces = []
        for b in range(blocks):
            above = (b * TILE - 8) % order
            below = (b + 1) * TILE % order
            strips = (
                (result[p, above : above + 8, band(b)], -8, 8),
                (result[p, band(b), band(b)], 0, TILE),
                (result[p, below : below + 8, band(b)], TILE, 8),
            )
            lines = [jnp.zeros((1, TILE), F32) for _ in range(2 * REACH + 1)]
            for block, base, height in strips:
                row = lax.broadcasted_iota(jnp.int32, (height, TILE), 0) + base
                offset = row - lax.broadcasted_iota(jnp.int32, (height, TILE), 1)
                for d in range(2 * REACH + 1):
                    lines[d] = lines[d] + jnp.sum(
                        jnp.where(offset == d - REACH, block, 0.0), axis=0, keepdims=True
                    )
            pieces.append(lines)
        return pieces

    def direct_terms():
        total = jnp.zeros((8, TILE), F32)
        group_of = lax.broadcasted_iota(jnp.int32, (padded, TILE), 0) // NHYP
        for p in range(steps):
            for b, lines in enumerate(diagonals(p)):
                matched = jnp.zeros((padded, TILE), F32)
                for d in range(2 * REACH + 1):
                    matched = jnp.where(group_of == d, lines[d], matched)
                terms = matched * weights[p, :, band(b)]
                for k in range(padded // 8):
                    total = total + terms[8 * k : 8 * (k + 1)]
        return total

    def exchange(k):
        other, where = peer(k)
        return pltpu.make_async_remote_copy(
            src_ref=partials.at[rank],
            dst_ref=partials.at[rank],
            send_sem=part_send.at[k],
            recv_sem=part_recv.at[rank],
            device_id=where,
            device_id_type=MESH,
        )

    def start_exchange(k, carry):
        exchange(k).start()
        return carry

    def prepare():
        mirror(result.at[0])
        partials[rank] = direct_terms()
        down = lax.broadcasted_iota(jnp.int32, (order, order), 0)
        offset = down - lax.broadcasted_iota(jnp.int32, (order, order), 1)

        def for_hyper(k, carry):
            for p in range(steps):
                gains = (c_hi[...], c_lo[...]) if p == 0 else (g_hi[p], g_lo[p])
                spots = jnp.zeros((order, order), F32)
                for d in range(-REACH, REACH + 1):
                    line = weights[p, pl.ds((d + REACH) * NHYP + k, 1), :]
                    here = offset == d
                    if d != 0:
                        here = jnp.logical_or(here, offset == (d - order if d > 0 else d + order))
                    spots = jnp.where(here, line, spots)
                right = product(split(spots), gains, NN)
                both = product(split(right.T), gains, NN)
                adjoint[k] = both if p == 0 else adjoint[k] + both
            return carry

        lax.fori_loop(0, NHYP, for_hyper, 0)

    def finish_early():
        total = partials[rank]
        spot = lax.broadcasted_iota(jnp.int32, (8, TILE), 0)
        current = b_hi[...].astype(F32) + b_lo[...].astype(F32)
        for k in range(NHYP):
            line = jnp.sum(adjoint[k] * current, axis=0, keepdims=True)
            line = sum(line[:, band(i)] for i in range(blocks))
            total = total + jnp.where(spot == k, line, 0.0)
        partials[rank] = total
        lax.fori_loop(1, group, start_exchange, 0)

    if early:

        @pl.when(me == 0)
        def _():
            prepare()

    if devices > 1:

        @pl.when(jnp.logical_not(is_last))
        def _():
            for i in range(blocks):
                hop(i).wait_recv()
                unpack(i)
                if i == 1:
                    first_half(c_hi, c_lo, 0)
                if i > 0 and not (early and i == blocks - 1):
                    first_half(c_hi, c_lo, i)
            if early:

                @pl.when(me == 0)
                def _():
                    finish_early()

                first_half(c_hi, c_lo, blocks - 1)
            for i in range(blocks):
                right = slice(i * TILE, order)
                fresh = second_half(c_hi, c_lo, result.at[0], i)
                result[0, band(i), right] = fresh

                @pl.when(me > 0)
                def _():
                    pack(i, result.at[0])
                    hop(i).start()

            for p in range(steps - 1, 0, -1):
                for i in range(blocks):
                    first_half(g_hi.at[p], g_lo.at[p], i)
                for i in range(blocks):
                    result[p, band(i), i * TILE :] = second_half(
                        g_hi.at[p], g_lo.at[p], s_in.at[p], i
                    )
                mirror(result.at[p])
                if p > 1:
                    set_current(result[p])

    if steps > 1 or devices > 1:
        mirror(result.at[0])

    if early:

        @pl.when(me != 0)
        def _():
            partials[rank] = direct_terms()
            lax.fori_loop(1, group, start_exchange, 0)
    else:
        partials[rank] = direct_terms()
        lax.fori_loop(1, group, start_exchange, 0)

    def take(k, carry):
        other, where = peer(k)
        pltpu.make_async_remote_copy(
            src_ref=partials.at[other],
            dst_ref=partials.at[other],
            send_sem=part_send.at[k],
            recv_sem=part_recv.at[other],
            device_id=where,
            device_id_type=MESH,
        ).wait_recv()
        return carry

    lax.fori_loop(1, group, take, 0)
    everything = jnp.sum(partials[...], axis=0)
    everything = everything[:NHYP] + everything[NHYP : 2 * NHYP]
    for k in range(NHYP):
        grad_ref[k] = -0.5 * jnp.sum(everything[k : k + 1])

    def finish_exchange(k, carry):
        exchange(k).wait_send()
        return carry

    lax.fori_loop(1, group, finish_exchange, 0)
    if devices > 1:

        @pl.when(jnp.logical_and(me > 0, jnp.logical_not(is_last)))
        def _():
            for i in range(blocks):
                hop(i).wait_send()

        if staggered:

            @pl.when(jnp.logical_and(is_last, jnp.logical_not(goes_first)))
            def _():
                for i in range(blocks):
                    hop(i).wait_send()


def on_device(group, coupling, schur_inverse, entry_rows, entry_shift, entry_hyper, entry_values):
    steps, _, order, _ = coupling.shape
    blocks = order // TILE
    whole = pl.BlockSpec(memory_space=pltpu.VMEM)
    apart = pl.BlockSpec(memory_space=pl.ANY)
    padded = 32
    entries = (entry_rows, entry_shift, entry_hyper, entry_values)
    travelling = [
        pltpu.VMEM((TILE, 2 * TILE), F32),
        pltpu.VMEM((TILE + 8, 2 * TILE), F32),
        pltpu.VMEM((TILE // 2 + 8, TILE), F32),
    ]
    return pl.pallas_call(
        kernel,
        out_shape=(
            OUT_TYPE(coupling.shape, F32),
            jax.ShapeDtypeStruct((NHYP,), F32),
        ),
        in_specs=[apart] * 6,
        out_specs=(whole, pl.BlockSpec(memory_space=pltpu.SMEM)),
        scratch_shapes=[
            pltpu.VMEM((steps, order, order), F32),
            pltpu.VMEM((steps, order, order), F32),
            *[pltpu.VMEM(x.shape, x.dtype) for x in entries],
            pltpu.VMEM((steps, order, order), BF16),
            pltpu.VMEM((steps, order, order), BF16),
            pltpu.VMEM((order, order), BF16),
            pltpu.VMEM((order, order), BF16),
            pltpu.VMEM((order, order), BF16),
            pltpu.VMEM((order, order), BF16),
            pltpu.VMEM((order, order), BF16),
            pltpu.VMEM((order, order), BF16),
            *travelling,
            *travelling,
            pltpu.VMEM((steps, padded, order), F32),
            pltpu.VMEM((NHYP, order, order), F32),
            pltpu.VMEM((group, 8, TILE), F32),
            pltpu.SemaphoreType.DMA((2, steps)),
            pltpu.SemaphoreType.DMA((len(entries),)),
            pltpu.SemaphoreType.DMA((blocks,)),
            pltpu.SemaphoreType.DMA((blocks,)),
            pltpu.SemaphoreType.REGULAR,
            pltpu.SemaphoreType.DMA((group,)),
            pltpu.SemaphoreType.DMA((group,)),
        ],
        compiler_params=pltpu.CompilerParams(collective_id=0, has_side_effects=True),
    )(coupling, schur_inverse, entry_rows, entry_shift, entry_hyper, entry_values)


def solution(mesh):
    group = mesh.shape["tm"] * mesh.shape["space"]
    in_specs = (
        P(("fits", "tm"), "space", None, None),
        P(("fits", "tm"), "space", None, None),
        P(("fits", "tm"), "space", None),
        P(("fits", "tm"), "space", None),
        P(("fits", "tm"), "space", None),
        P(("fits", "tm"), "space", None),
    )
    out_specs = (P(("fits", "tm"), "space", None, None), P("fits"))
    return jax.shard_map(
        functools.partial(on_device, group),
        mesh=mesh,
        in_specs=in_specs,
        out_specs=out_specs,
        check_vma=False,
    )
```
